32 devices in a mesh: replica: 4 (over y, x), fsdp: 8 (over z, core).
Axes of the slice: x: 2, y: 2, z: 4, core: 2. Of those that a mesh axis runs over, the one named last changes fastest.
Arguments:
- local_weights: bfloat16 [4, 256, 28672], P('replica', 'fsdp'), may hold values from -6 to 6
- base_weights: float32 [256, 28672], P('fsdp'), may hold values from -6 to 6
- momentum: float32 [256, 28672], P('replica', 'fsdp'), may hold values from -4 to 4
Outputs:
- new_weights: float32 [256, 28672], P('fsdp')
- new_momentum: float32 [256, 28672], P('replica', 'fsdp')
The draws below stay inside these ranges and needn't reach their ends.
All inputs are finite; a program needn't handle non-finite values. Where the reference program divides by a largest or mean magnitude, that divisor is 1e-20 or more.
Results may differ from the reference program's by a relative error of at most 0.015.
Values may be sent and summed in bfloat16 or wider, within the bound.
A program may use at most 128 MiB of HBM per device.

```python
import jax
import jax.numpy as jnp

FF = 28672
QBLOCK = 128
REPLICAS = 4
ROWS = 256


def block_levels(rng, shape, shards, smallest, top_value):
    level, own = 1.0, jax.random.fold_in(rng, 6)
    for dim, shards_of in shards:
        steps = jnp.exp(jax.random.uniform(jax.random.fold_in(own, dim), (shards_of,), jnp.float32, smallest / len(shards), top_value / len(shards)))
        level = level * jnp.repeat(steps, shape[dim] // shards_of).reshape([-1 if axis == dim else 1 for axis in range(len(shape))])
    return level


def gaussian(key, dims, spread, most, split=(), dtype=jnp.bfloat16):
    drawn = spread * jax.random.normal(key, dims, jnp.float32)
    if split:
        drawn = drawn * block_levels(key, dims, split, -0.22, 0.18)
    return jnp.clip(drawn, -most, most).astype(dtype)


def setup_inputs(seed: int = 0) -> dict:
    seeds = jax.random.split(jax.random.key(seed), 4)
    return {
        "local_weights": gaussian(seeds[0], (REPLICAS, ROWS, FF), 1.0, 6.0, ((0, 4), (1, 8))),
        "base_weights": gaussian(seeds[1], (ROWS, FF), 1.0, 6.0, ((0, 8),), jnp.float32),
        "momentum": gaussian(seeds[2], (ROWS, FF), 0.5, 4.0, ((0, 4), (1, 8)), jnp.float32),
    }


EPSILON = 1e-6
LEARN_RATE = 0.7
MOMENTUM_COEF = 0.9


def block_quantize(replica_differences):
    row_count = replica_differences.shape[0]
    block_grouped = replica_differences.reshape(row_count, -1, QBLOCK)
    block_scales = (jnp.max(jnp.abs(block_grouped), axis=2) + EPSILON).astype(jnp.bfloat16)
    integer_levels = (block_grouped / block_scales.astype(jnp.float32)[:, :, None]).astype(jnp.bfloat16)
    return integer_levels, block_scales


def reference(local_weights, base_weights, momentum):
    total = jnp.zeros(base_weights.shape, jnp.float32)
    for replica in range(REPLICAS):
        replica_differences = base_weights - local_weights[replica].astype(jnp.float32)
        integer_levels, block_scales = block_quantize(replica_differences)
        values = integer_levels.astype(jnp.float32) * block_scales.astype(jnp.float32)[:, :, None]
        total = total + values.reshape(base_weights.shape)
    average = total / REPLICAS
    new_momentum = MOMENTUM_COEF * momentum + average
    update = (LEARN_RATE * (average + MOMENTUM_COEF * new_momentum)).astype(jnp.bfloat16)
    new_weights = base_weights - update.astype(jnp.float32)
    return new_weights, new_momentum
```

```python
import functools

import jax
import jax.numpy as jnp
from jax import lax
from jax.experimental import pallas as pl
from jax.experimental.pallas import tpu as pltpu
from jax.sharding import PartitionSpec as P

LANES = 128
LEARN_RATE = 0.7
MOMENTUM_COEF = 0.9
MESH = pl.DeviceIdType.MESH


def sync_kernel(
    replicas, group, per,
    local, base, mom, gathered, avg_home,
    loc_recv, base_own, m_recv, u_own, avg_own,
    rs_send, rs_recv, m_send_sem, m_recv_sem, ag_send, ag_recv, h_send, h_recv, own_sem, base_sem, out_sem,
):
    r = lax.axis_index("replica")
    f = lax.axis_index("fsdp")
    rows, cols = local.shape
    quarter = cols // replicas
    piece = mom.shape[1]
    width = piece // per
    chunks = group * per
    line = f // group
    sub = f % group
    diagonal = line == r

    def span(start):
        return pl.ds(pl.multiple_of(start, LANES), width)

    def side(k):
        return r * group + k

    own, own_base = [], []
    for c in range(chunks):
        at = span(r * quarter + c * width)
        own.append(pltpu.make_async_copy(local.at[:, at], loc_recv.at[0, :, pl.ds(c * width, width)], own_sem.at[c]))
        own_base.append(pltpu.make_async_copy(base.at[:, at], base_own.at[:, pl.ds(c * width, width)], base_sem.at[c]))
    for c in range(chunks):
        own[c].start()
        own_base[c].start()

    barrier = pltpu.get_barrier_semaphore()
    for d in range(1, replicas):
        pl.semaphore_signal(barrier, inc=1, device_id={"replica": r ^ d}, device_id_type=MESH)
    for k in range(group):
        @pl.when(jnp.logical_or(line != r, sub != k))
        def _():
            pl.semaphore_signal(barrier, inc=1, device_id={"replica": line, "fsdp": side(k)}, device_id_type=MESH)
    pl.semaphore_wait(barrier, replicas - 1 + group - diagonal.astype(jnp.int32))

    def m_copies(k, i):
        src = mom.at[pl.ds(k * rows, rows), pl.ds(i * width, width)]
        dst = m_recv.at[:, span(sub * piece + i * width)]
        arrived = m_recv_sem.at[sub * per + i]
        return (
            pltpu.make_async_remote_copy(
                src_ref=src, dst_ref=dst, send_sem=m_send_sem.at[k * per + i], recv_sem=arrived,
                device_id={"replica": line, "fsdp": side(k)}, device_id_type=MESH),
            pltpu.make_async_copy(src, dst, arrived),
        )

    def h_copies(c):
        j, i = divmod(c, per)
        src = avg_own.at[:, pl.ds(c * width, width)]
        dst = avg_home.at[pl.ds(pl.multiple_of(sub * rows, rows), rows), pl.ds(i * width, width)]
        arrived = h_recv.at[sub * per + i]
        return (
            pltpu.make_async_remote_copy(
                src_ref=src, dst_ref=dst, send_sem=h_send.at[c], recv_sem=arrived,
                device_id={"replica": line, "fsdp": side(j)}, device_id_type=MESH),
            pltpu.make_async_copy(src, dst, arrived),
        )

    def elsewhere(k):
        return jnp.logical_or(line != r, sub != k)

    def start(pair, k):
        far, near = pair
        pl.when(elsewhere(k))(far.start)
        pl.when(jnp.logical_not(elsewhere(k)))(near.start)

    def wait_sent(pair, k):
        pl.when(elsewhere(k))(pair[0].wait_send)

    def rs_copy(d, c):
        t = r ^ d
        return pltpu.make_async_remote_copy(
            src_ref=local.at[:, span(t * quarter + c * width)],
            dst_ref=loc_recv.at[d, :, pl.ds(c * width, width)],
            send_sem=rs_send.at[d - 1, c], recv_sem=rs_recv.at[d - 1, c],
            device_id={"replica": t}, device_id_type=MESH)

    def ag_copy(d, c):
        return pltpu.make_async_remote_copy(
            src_ref=u_own.at[:, pl.ds(c * width, width)],
            dst_ref=gathered.at[:, span(r * quarter + c * width)],
            send_sem=ag_send.at[d - 1, c], recv_sem=ag_recv.at[d - 1, c],
            device_id={"replica": r ^ d}, device_id_type=MESH)

    order = list(range(replicas - 1, 0, -1))
    for i in range(per):
        for k in range(group):
            start(m_copies(k, i), k)
    for c in range(chunks):
        for d in order:
            rs_copy(d, c).start()

    def wait_bytes(ref, sem):
        pltpu.make_async_copy(ref, ref, sem).wait()

    outs = []
    for c in range(chunks):
        here = pl.ds(c * width, width)
        own[c].wait()
        own_base[c].wait()
        for d in order:
            rs_copy(d, c).wait_recv()
        wait_bytes(m_recv.at[:, here], m_recv_sem.at[c])
        total = loc_recv[0, :, here].astype(jnp.float32)
        for d in range(1, replicas):
            total = total + loc_recv[d, :, here].astype(jnp.float32)
        average = base_own[:, here] - total * (1.0 / replicas)
        new = MOMENTUM_COEF * m_recv[:, here].astype(jnp.float32) + average
        update = LEARN_RATE * (average + MOMENTUM_COEF * new)
        u_own[:, here] = update.astype(jnp.bfloat16)
        avg_own[:, here] = average.astype(jnp.bfloat16)
        for d in order:
            ag_copy(d, c).start()
        start(h_copies(c), c // per)
        out = pltpu.make_async_copy(u_own.at[:, here], gathered.at[:, span(r * quarter + c * width)], out_sem.at[c])
        out.start()
        outs.append(out)

    for c in range(chunks):
        for d in order:
            ag_copy(d, c).wait_recv()
    for k in range(group):
        for i in range(per):
            wait_bytes(avg_home.at[pl.ds(k * rows, rows), pl.ds(i * width, width)], h_recv.at[k * per + i])
    for c in range(chunks):
        outs[c].wait()
        for d in order:
            rs_copy(d, c).wait_send()
            ag_copy(d, c).wait_send()
        wait_sent(h_copies(c), c // per)
    for i in range(per):
        for k in range(group):
            wait_sent(m_copies(k, i), k)


def per_device(local_weights, base_weights, momentum):
    rows, cols = base_weights.shape
    replicas = lax.axis_size("replica")
    group = lax.axis_size("fsdp") // replicas
    piece = momentum.shape[1]
    per = 2 if piece % (2 * LANES) == 0 else 1
    chunks = group * per
    quarter = cols // replicas
    dma = pltpu.SemaphoreType.DMA
    gathered, avg_home = pl.pallas_call(
        functools.partial(sync_kernel, replicas, group, per),
        out_shape=(
            jax.ShapeDtypeStruct((rows, cols), jnp.bfloat16),
            jax.ShapeDtypeStruct(momentum.shape, jnp.bfloat16),
        ),
        in_specs=[pl.BlockSpec(memory_space=pl.ANY)] * 3,
        out_specs=(pl.BlockSpec(memory_space=pl.ANY),) * 2,
        scratch_shapes=[
            pltpu.VMEM((replicas, rows, quarter), jnp.bfloat16),
            pltpu.VMEM((rows, quarter), jnp.float32),
            pltpu.VMEM((rows, quarter), jnp.bfloat16),
            pltpu.VMEM((rows, quarter), jnp.bfloat16),
            pltpu.VMEM((rows, quarter), jnp.bfloat16),
            dma((replicas - 1, chunks)), dma((replicas - 1, chunks)),
            dma((chunks,)), dma((chunks,)),
            dma((replicas - 1, chunks)), dma((replicas - 1, chunks)),
            dma((chunks,)), dma((chunks,)),
            dma((chunks,)), dma((chunks,)), dma((chunks,)),
        ],
        compiler_params=pltpu.CompilerParams(collective_id=0, has_side_effects=True),
    )(local_weights[0], base_weights, momentum.astype(jnp.bfloat16))
    new_weights = base_weights - gathered.astype(jnp.float32)
    new_momentum = MOMENTUM_COEF * momentum + avg_home.astype(jnp.float32)
    return new_weights, new_momentum


def solution(mesh):
    return jax.shard_map(
        per_device,
        mesh=mesh,
        in_specs=(P("replica", "fsdp", None), P("fsdp", None), P("replica", "fsdp")),
        out_specs=(P("fsdp", None), P("replica", "fsdp")),
        check_vma=False,
    )
```

```python
import functools

import jax
import jax.numpy as jnp
from jax import lax
from jax.experimental import pallas as pl
from jax.experimental.pallas import tpu as pltpu
from jax.sharding import PartitionSpec as P

LANES = 128
LEARN_RATE = 0.7
MOMENTUM_COEF = 0.9
MESH = pl.DeviceIdType.MESH
AHEAD = 2
LAG = 2


def sync_kernel(
    replicas, shards, per,
    local, base, mom, gathered, u_home,
    base_vm, loc_vm, m_recv, fold, loc_recv, u_own, total,
    rs_send, rs_recv, m_send, m_arrived, ag_send, ag_recv, h_send, h_recv, load_sem, out_sem,
):
    r = lax.axis_index("replica")
    f = lax.axis_index("fsdp")
    group = shards // replicas
    rows, cols = local.shape
    quarter = cols // replicas
    piece = mom.shape[1]
    width = piece // per
    line = f // group
    sub = f % group
    hub = line == r
    fold_coef = replicas * MOMENTUM_COEF * MOMENTUM_COEF / (1.0 + MOMENTUM_COEF)
    steps = [(i, j) for i in range(per) for j in range(group)]

    def span(start):
        return pl.ds(pl.multiple_of(start, LANES), width)

    load_local = pltpu.make_async_copy(local, loc_vm, load_sem.at[0])
    load_base = pltpu.make_async_copy(base, base_vm, load_sem.at[1])
    load_local.start()
    load_base.start()

    barrier = pltpu.get_barrier_semaphore()
    for d in range(1, replicas):
        pl.semaphore_signal(barrier, inc=1, device_id={"replica": r ^ d}, device_id_type=MESH)
    for e in range(1, shards):
        other = f ^ e

        @pl.when(jnp.logical_or(hub, other // group == r))
        def _():
            pl.semaphore_signal(barrier, inc=1, device_id={"fsdp": other}, device_id_type=MESH)

    pl.semaphore_wait(barrier, replicas - 1 + jnp.where(hub, shards - 1, group))

    def m_far(k, i):
        return pltpu.make_async_remote_copy(
            src_ref=mom.at[pl.ds(k * rows, rows), pl.ds(i * width, width)],
            dst_ref=m_recv.at[:, span(f * piece + i * width)],
            send_sem=m_send.at[k * per + i], recv_sem=m_arrived.at[f * per + i],
            device_id={"fsdp": r * group + k}, device_id_type=MESH)

    def m_near(k, i):
        return pltpu.make_async_copy(
            mom.at[pl.ds(k * rows, rows), pl.ds(i * width, width)],
            m_recv.at[:, span(f * piece + i * width)], m_arrived.at[f * per + i])

    def rs_copy(d, i, j, source):
        c = j * per + i
        return pltpu.make_async_remote_copy(
            src_ref=source.at[:, span((r ^ d) * quarter + c * width)],
            dst_ref=loc_recv.at[d - 1, :, pl.ds(c * width, width)],
            send_sem=rs_send.at[d - 1, c], recv_sem=rs_recv.at[d - 1, c],
            device_id={"replica": r ^ d}, device_id_type=MESH)

    def ag_copy(d, i, j):
        c = j * per + i
        return pltpu.make_async_remote_copy(
            src_ref=u_own.at[:, pl.ds(c * width, width)],
            dst_ref=gathered.at[:, span(r * quarter + c * width)],
            send_sem=ag_send.at[d - 1, c], recv_sem=ag_recv.at[d - 1, c],
            device_id={"replica": r ^ d}, device_id_type=MESH)

    def h_source(d, i, j):
        c = j * per + i
        if d == 0:
            return u_own.at[:, pl.ds(c * width, width)]
        return gathered.at[:, span((r ^ d) * quarter + c * width)]

    def h_target(i):
        return u_home.at[pl.ds(pl.multiple_of(sub * rows, rows), rows), pl.ds(i * width, width)]

    def h_far(d, i, j):
        return pltpu.make_async_remote_copy(
            src_ref=h_source(d, i, j), dst_ref=h_target(i),
            send_sem=h_send.at[d, j * per + i], recv_sem=h_recv.at[sub * per + i],
            device_id={"fsdp": (r ^ d) * group + j}, device_id_type=MESH)

    def h_near(i, j):
        return pltpu.make_async_copy(h_source(0, i, j), h_target(i), h_recv.at[sub * per + i])

    def wait_bytes(ref, sem):
        pltpu.make_async_copy(ref, ref, sem).wait()

    order = list(range(replicas - 1, 0, -1))

    def send_local(i, j):
        @pl.when(jnp.logical_not(hub))
        def _():
            for d in order:
                rs_copy(d, i, j, local).start()

    def send_fold(i, j):
        @pl.when(hub)
        def _():
            for d in [0] + order[::-1]:
                side = (r ^ d) * group + j
                at = span(side * piece + i * width)
                wait_bytes(m_recv.at[:, at], m_arrived.at[side * per + i])
                if d:
                    delta = base_vm[:, at] - loc_vm[:, at].astype(jnp.float32)
                    fold[:, at] = (delta + fold_coef * m_recv[:, at].astype(jnp.float32)).astype(jnp.bfloat16)
                    rs_copy(d, i, j, fold).start()

    def reduce(i, j):
        c = j * per + i
        here = pl.ds(c * width, width)
        at = span(r * quarter + c * width)
        own_base = base_vm[:, at]
        total[...] = own_base - loc_vm[:, at].astype(jnp.float32)

        @pl.when(hub)
        def _():
            total[...] += fold_coef * m_recv[:, at].astype(jnp.float32)

        for d in order:
            rs_copy(d, i, j, local).wait_recv()
        summed = total[...]
        for d in range(1, replicas):
            came = loc_recv[d - 1, :, here].astype(jnp.float32)
            summed = summed + jnp.where((r ^ d) == line, came, own_base - came)
        scale = LEARN_RATE * (1.0 + MOMENTUM_COEF) / replicas
        u_own[:, here] = (scale * summed).astype(jnp.bfloat16)
        for d in order:
            ag_copy(d, i, j).start()

        @pl.when(jnp.logical_and(hub, sub != j))
        def _():
            h_far(0, i, j).start()

        @pl.when(jnp.logical_and(hub, sub == j))
        def _():
            h_near(i, j).start()

        out_copy(i, j).start()

    def out_copy(i, j):
        c = j * per + i
        return pltpu.make_async_copy(
            u_own.at[:, pl.ds(c * width, width)], gathered.at[:, span(r * quarter + c * width)], out_sem.at[c])

    def give_back(i, j):
        for d in order[::-1]:
            ag_copy(d, i, j).wait_recv()

            @pl.when(hub)
            def _():
                h_far(d, i, j).start()

    for i in range(per):
        for k in range(group):
            away = f != r * group + k

            @pl.when(away)
            def _():
                m_far(k, i).start()

            @pl.when(jnp.logical_not(away))
            def _():
                m_near(k, i).start()

    for s in range(min(AHEAD, len(steps))):
        send_local(*steps[s])
    load_local.wait()
    load_base.wait()
    for s in range(len(steps) + LAG):
        if s + AHEAD < len(steps):
            send_local(*steps[s + AHEAD])
        if s < len(steps):
            send_fold(*steps[s])
            reduce(*steps[s])
        if s >= LAG:
            give_back(*steps[s - LAG])

    for k in range(group):
        for i in range(per):
            wait_bytes(u_home.at[pl.ds(k * rows, rows), pl.ds(i * width, width)], h_recv.at[k * per + i])

            @pl.when(f != r * group + k)
            def _():
                m_far(k, i).wait_send()

    for i, j in steps:
        out_copy(i, j).wait()
        for d in order:
            rs_copy(d, i, j, local).wait_send()
            ag_copy(d, i, j).wait_send()

        @pl.when(hub)
        def _():
            for d in order:
                h_far(d, i, j).wait_send()

        @pl.when(jnp.logical_and(hub, sub != j))
        def _():
            h_far(0, i, j).wait_send()


def per_device(local_weights, base_weights, momentum):
    rows, cols = base_weights.shape
    replicas = lax.axis_size("replica")
    shards = lax.axis_size("fsdp")
    group = shards // replicas
    piece = momentum.shape[1]
    per = next(n for n in (4, 2, 1) if piece % (n * LANES) == 0)
    chunks = group * per
    quarter = cols // replicas
    dma = pltpu.SemaphoreType.DMA
    gathered, u_home = pl.pallas_call(
        functools.partial(sync_kernel, replicas, shards, per),
        out_shape=(
            jax.ShapeDtypeStruct((rows, cols), jnp.bfloat16),
            jax.ShapeDtypeStruct(momentum.shape, jnp.bfloat16),
        ),
        in_specs=[pl.BlockSpec(memory_space=pl.ANY)] * 3,
        out_specs=(pl.BlockSpec(memory_space=pl.ANY),) * 2,
        scratch_shapes=[
            pltpu.VMEM((rows, cols), jnp.float32),
            pltpu.VMEM((rows, cols), jnp.bfloat16),
            pltpu.VMEM((rows, cols), jnp.bfloat16),
            pltpu.VMEM((rows, cols), jnp.bfloat16),
            pltpu.VMEM((replicas - 1, rows, quarter), jnp.bfloat16),
            pltpu.VMEM((rows, quarter), jnp.bfloat16),
            pltpu.VMEM((rows, piece // per), jnp.float32),
            dma((replicas - 1, chunks)), dma((replicas - 1, chunks)),
            dma((group * per,)), dma((shards * per,)),
            dma((replicas - 1, chunks)), dma((replicas - 1, chunks)),
            dma((replicas, chunks)), dma((group * per,)),
            dma((2,)), dma((chunks,)),
        ],
        compiler_params=pltpu.CompilerParams(
            collective_id=0, has_side_effects=True, vmem_limit_bytes=48 * 1024 * 1024),
    )(local_weights[0], base_weights, momentum.astype(jnp.bfloat16))
    new_weights = base_weights - gathered.astype(jnp.float32)
    new_momentum = (MOMENTUM_COEF * momentum + unscaled(u_home)) / (1.0 + MOMENTUM_COEF)
    return new_weights, new_momentum


def unscaled(update):
    return update.astype(jnp.float32) / LEARN_RATE


def solution(mesh):
    return jax.shard_map(
        per_device,
        mesh=mesh,
        in_specs=(P("replica", "fsdp", None), P("fsdp", None), P("replica", "fsdp")),
        out_specs=(P("fsdp", None), P("replica", "fsdp")),
        check_vma=False,
    )
```

```python
import functools

import jax
import jax.numpy as jnp
from jax import lax
from jax.experimental import pallas as pl
from jax.experimental.pallas import tpu as pltpu
from jax.sharding import PartitionSpec as P

LANES = 128
LEARN_RATE = 0.7
MOMENTUM_COEF = 0.9
MESH = pl.DeviceIdType.MESH
AHEAD = 2
LAG = 2


def sync_kernel(
    replicas, shards, per,
    local, base, mom_full, gathered, u_home,
    base_vm, loc_vm, mom_vm, mom, m_recv, fold, loc_recv, u_own, total,
    rs_send, rs_recv, m_send, m_arrived, ag_send, ag_recv, h_send, h_recv, load_sem, out_sem,
):
    r = lax.axis_index("replica")
    f = lax.axis_index("fsdp")
    group = shards // replicas
    rows, cols = local.shape
    quarter = cols // replicas
    piece = mom.shape[1]
    width = piece // per
    line = f // group
    sub = f % group
    hub = line == r
    fold_coef = replicas * MOMENTUM_COEF * MOMENTUM_COEF / (1.0 + MOMENTUM_COEF)
    steps = [(i, j) for i in range(per) for j in range(group)]

    def span(start):
        return pl.ds(pl.multiple_of(start, LANES), width)

    load_local = pltpu.make_async_copy(local, loc_vm, load_sem.at[0])
    load_base = pltpu.make_async_copy(base, base_vm, load_sem.at[1])
    load_local.start()
    load_base.start()
    load_mom = pltpu.make_async_copy(mom_full, mom_vm, load_sem.at[2])
    load_mom.start()

    barrier = pltpu.get_barrier_semaphore()
    for d in range(1, replicas):
        pl.semaphore_signal(barrier, inc=1, device_id={"replica": r ^ d}, device_id_type=MESH)
    for e in range(1, shards):
        other = f ^ e

        @pl.when(jnp.logical_or(hub, other // group == r))
        def _():
            pl.semaphore_signal(barrier, inc=1, device_id={"fsdp": other}, device_id_type=MESH)

    load_mom.wait()
    mom[...] = mom_vm[...].astype(jnp.bfloat16)
    pl.semaphore_wait(barrier, replicas - 1 + jnp.where(hub, shards - 1, group))

    def m_far(k, i):
        return pltpu.make_async_remote_copy(
            src_ref=mom.at[pl.ds(k * rows, rows), pl.ds(i * width, width)],
            dst_ref=m_recv.at[:, span(f * piece + i * width)],
            send_sem=m_send.at[k * per + i], recv_sem=m_arrived.at[f * per + i],
            device_id={"fsdp": r * group + k}, device_id_type=MESH)

    def m_near(k, i):
        return pltpu.make_async_copy(
            mom.at[pl.ds(k * rows, rows), pl.ds(i * width, width)],
            m_recv.at[:, span(f * piece + i * width)], m_arrived.at[f * per + i])

    def rs_copy(d, i, j, source):
        c = j * per + i
        return pltpu.make_async_remote_copy(
            src_ref=source.at[:, span((r ^ d) * quarter + c * width)],
            dst_ref=loc_recv.at[d - 1, :, pl.ds(c * width, width)],
            send_sem=rs_send.at[d - 1, c], recv_sem=rs_recv.at[d - 1, c],
            device_id={"replica": r ^ d}, device_id_type=MESH)

    def ag_copy(d, i, j):
        c = j * per + i
        return pltpu.make_async_remote_copy(
            src_ref=u_own.at[:, pl.ds(c * width, width)],
            dst_ref=gathered.at[:, span(r * quarter + c * width)],
            send_sem=ag_send.at[d - 1, c], recv_sem=ag_recv.at[d - 1, c],
            device_id={"replica": r ^ d}, device_id_type=MESH)

    def h_source(d, i, j):
        c = j * per + i
        if d == 0:
            return u_own.at[:, pl.ds(c * width, width)]
        return gathered.at[:, span((r ^ d) * quarter + c * width)]

    def h_target(i):
        return u_home.at[pl.ds(pl.multiple_of(sub * rows, rows), rows), pl.ds(i * width, width)]

    def h_far(d, i, j):
        return pltpu.make_async_remote_copy(
            src_ref=h_source(d, i, j), dst_ref=h_target(i),
            send_sem=h_send.at[d, j * per + i], recv_sem=h_recv.at[sub * per + i],
            device_id={"fsdp": (r ^ d) * group + j}, device_id_type=MESH)

    def h_near(i, j):
        return pltpu.make_async_copy(h_source(0, i, j), h_target(i), h_recv.at[sub * per + i])

    def wait_bytes(ref, sem):
        pltpu.make_async_copy(ref, ref, sem).wait()

    order = list(range(replicas - 1, 0, -1))

    def send_local(i, j):
        @pl.when(jnp.logical_not(hub))
        def _():
            for d in order:
                rs_copy(d, i, j, local).start()

    def send_fold(i, j):
        @pl.when(hub)
        def _():
            for d in [0] + order[::-1]:
                side = (r ^ d) * group + j
                at = span(side * piece + i * width)
                wait_bytes(m_recv.at[:, at], m_arrived.at[side * per + i])
                if d:
                    delta = base_vm[:, at] - loc_vm[:, at].astype(jnp.float32)
                    fold[:, at] = (delta + fold_coef * m_recv[:, at].astype(jnp.float32)).astype(jnp.bfloat16)
                    rs_copy(d, i, j, fold).start()

    def reduce(i, j):
        c = j * per + i
        here = pl.ds(c * width, width)
        at = span(r * quarter + c * width)
        own_base = base_vm[:, at]
        total[...] = own_base - loc_vm[:, at].astype(jnp.float32)

        @pl.when(hub)
        def _():
            total[...] += fold_coef * m_recv[:, at].astype(jnp.float32)

        for d in order:
            rs_copy(d, i, j, local).wait_recv()
        summed = total[...]
        for d in range(1, replicas):
            came = loc_recv[d - 1, :, here].astype(jnp.float32)
            summed = summed + jnp.where((r ^ d) == line, came, own_base - came)
        scale = LEARN_RATE * (1.0 + MOMENTUM_COEF) / replicas
        u_own[:, here] = (scale * summed).astype(jnp.bfloat16)
        for d in order:
            ag_copy(d, i, j).start()

        @pl.when(jnp.logical_and(hub, sub != j))
        def _():
            h_far(0, i, j).start()

        @pl.when(jnp.logical_and(hub, sub == j))
        def _():
            h_near(i, j).start()

        out_copy(i, j).start()

    def out_copy(i, j):
        c = j * per + i
        return pltpu.make_async_copy(
            u_own.at[:, pl.ds(c * width, width)], gathered.at[:, span(r * quarter + c * width)], out_sem.at[c])

    def give_back(i, j):
        for d in order[::-1]:
            ag_copy(d, i, j).wait_recv()

            @pl.when(hub)
            def _():
                h_far(d, i, j).start()

    def send_momentum(i):
        for k in range(group):
            away = f != r * group + k

            @pl.when(away)
            def _():
                m_far(k, i).start()

            @pl.when(jnp.logical_not(away))
            def _():
                m_near(k, i).start()

    for s in range(min(AHEAD, len(steps))):
        if s < per:
            send_momentum(s)
        send_local(*steps[s])
    load_local.wait()
    load_base.wait()
    for s in range(len(steps) + LAG):
        if s % group == 0 and AHEAD <= s // group + AHEAD < per:
            send_momentum(s // group + AHEAD)
        if s + AHEAD < len(steps):
            send_local(*steps[s + AHEAD])
        if s < len(steps):
            send_fold(*steps[s])
            reduce(*steps[s])
        if s >= LAG:
            give_back(*steps[s - LAG])

    for k in range(group):
        for i in range(per):
            wait_bytes(u_home.at[pl.ds(k * rows, rows), pl.ds(i * width, width)], h_recv.at[k * per + i])

            @pl.when(f != r * group + k)
            def _():
                m_far(k, i).wait_send()

    for i, j in steps:
        out_copy(i, j).wait()
        for d in order:
            rs_copy(d, i, j, local).wait_send()
            ag_copy(d, i, j).wait_send()

        @pl.when(hub)
        def _():
            for d in order:
                h_far(d, i, j).wait_send()

        @pl.when(jnp.logical_and(hub, sub != j))
        def _():
            h_far(0, i, j).wait_send()


def per_device(local_weights, base_weights, momentum):
    rows, cols = base_weights.shape
    replicas = lax.axis_size("replica")
    shards = lax.axis_size("fsdp")
    group = shards // replicas
    piece = momentum.shape[1]
    per = next(n for n in (4, 2, 1) if piece % (n * LANES) == 0)
    chunks = group * per
    quarter = cols // replicas
    dma = pltpu.SemaphoreType.DMA
    gathered, u_home = pl.pallas_call(
        functools.partial(sync_kernel, replicas, shards, per),
        out_shape=(
            jax.ShapeDtypeStruct((rows, cols), jnp.bfloat16),
            jax.ShapeDtypeStruct(momentum.shape, jnp.bfloat16),
        ),
        in_specs=[pl.BlockSpec(memory_space=pl.ANY)] * 3,
        out_specs=(pl.BlockSpec(memory_space=pl.ANY),) * 2,
        scratch_shapes=[
            pltpu.VMEM((rows, cols), jnp.float32),
            pltpu.VMEM((rows, cols), jnp.bfloat16),
            pltpu.VMEM(momentum.shape, jnp.float32),
            pltpu.VMEM(momentum.shape, jnp.bfloat16),
            pltpu.VMEM((rows, cols), jnp.bfloat16),
            pltpu.VMEM((rows, cols), jnp.bfloat16),
            pltpu.VMEM((replicas - 1, rows, quarter), jnp.bfloat16),
            pltpu.VMEM((rows, quarter), jnp.bfloat16),
            pltpu.VMEM((rows, piece // per), jnp.float32),
            dma((replicas - 1, chunks)), dma((replicas - 1, chunks)),
            dma((group * per,)), dma((shards * per,)),
            dma((replicas - 1, chunks)), dma((replicas - 1, chunks)),
            dma((replicas, chunks)), dma((group * per,)),
            dma((3,)), dma((chunks,)),
        ],
        compiler_params=pltpu.CompilerParams(
            collective_id=0, has_side_effects=True, vmem_limit_bytes=48 * 1024 * 1024),
    )(local_weights[0], base_weights, momentum)
    new_weights = base_weights - gathered.astype(jnp.float32)
    new_momentum = (MOMENTUM_COEF * momentum + unscaled(u_home)) / (1.0 + MOMENTUM_COEF)
    return new_weights, new_momentum


def unscaled(update):
    return update.astype(jnp.float32) / LEARN_RATE


def solution(mesh):
    return jax.shard_map(
        per_device,
        mesh=mesh,
        in_specs=(P("replica", "fsdp", None), P("fsdp", None), P("replica", "fsdp")),
        out_specs=(P("fsdp", None), P("replica", "fsdp")),
        check_vma=False,
    )
```

```python
import functools

import jax
import jax.numpy as jnp
from jax import lax
from jax.experimental import pallas as pl
from jax.experimental.pallas import tpu as pltpu
from jax.sharding import PartitionSpec as P

LANES = 128
LEARN_RATE = 0.7
MOMENTUM_COEF = 0.9
MESH = pl.DeviceIdType.MESH
AHEAD = 3
LAG = 3
M_AHEAD = 1


def sync_kernel(
    replicas, shards, per,
    local, base, mom_full, gathered, u_home,
    base_vm, loc_vm, mom_vm, mom, m_recv, fold, loc_recv, u_own, total,
    rs_send, rs_recv, m_send, m_arrived, ag_send, ag_recv, h_send, h_recv, load_sem, out_sem,
):
    r = lax.axis_index("replica")
    f = lax.axis_index("fsdp")
    group = shards // replicas
    rows, cols = local.shape
    quarter = cols // replicas
    piece = mom.shape[1]
    width = piece // per
    line = f // group
    sub = f % group
    hub = line == r
    fold_coef = replicas * MOMENTUM_COEF * MOMENTUM_COEF / (1.0 + MOMENTUM_COEF)
    steps = [(i, j) for i in range(per) for j in range(group)]

    def span(start):
        return pl.ds(pl.multiple_of(start, LANES), width)

    load_local = pltpu.make_async_copy(local, loc_vm, load_sem.at[0])
    load_base = pltpu.make_async_copy(base, base_vm, load_sem.at[1])
    load_local.start()
    load_base.start()
    load_mom = pltpu.make_async_copy(mom_full, mom_vm, load_sem.at[2])
    load_mom.start()

    barrier = pltpu.get_barrier_semaphore()
    for d in range(1, replicas):
        pl.semaphore_signal(barrier, inc=1, device_id={"replica": r ^ d}, device_id_type=MESH)
    for e in range(1, shards):
        other = f ^ e

        @pl.when(jnp.logical_or(hub, other // group == r))
        def _():
            pl.semaphore_signal(barrier, inc=1, device_id={"fsdp": other}, device_id_type=MESH)

    load_mom.wait()
    mom[...] = mom_vm[...].astype(jnp.bfloat16)
    pl.semaphore_wait(barrier, replicas - 1 + jnp.where(hub, shards - 1, group))

    def m_far(k, i):
        return pltpu.make_async_remote_copy(
            src_ref=mom.at[pl.ds(k * rows, rows), pl.ds(i * width, width)],
            dst_ref=m_recv.at[:, span(f * piece + i * width)],
            send_sem=m_send.at[k * per + i], recv_sem=m_arrived.at[f * per + i],
            device_id={"fsdp": r * group + k}, device_id_type=MESH)

    def m_near(k, i):
        return pltpu.make_async_copy(
            mom.at[pl.ds(k * rows, rows), pl.ds(i * width, width)],
            m_recv.at[:, span(f * piece + i * width)], m_arrived.at[f * per + i])

    def rs_copy(d, i, j, source):
        c = j * per + i
        return pltpu.make_async_remote_copy(
            src_ref=source.at[:, span((r ^ d) * quarter + c * width)],
            dst_ref=loc_recv.at[d - 1, :, pl.ds(c * width, width)],
            send_sem=rs_send.at[d - 1, c], recv_sem=rs_recv.at[d - 1, c],
            device_id={"replica": r ^ d}, device_id_type=MESH)

    def ag_copy(d, i, j):
        c = j * per + i
        return pltpu.make_async_remote_copy(
            src_ref=u_own.at[:, pl.ds(c * width, width)],
            dst_ref=gathered.at[:, span(r * quarter + c * width)],
            send_sem=ag_send.at[d - 1, c], recv_sem=ag_recv.at[d - 1, c],
            device_id={"replica": r ^ d}, device_id_type=MESH)

    def h_source(d, i, j):
        c = j * per + i
        if d == 0:
            return u_own.at[:, pl.ds(c * width, width)]
        return gathered.at[:, span((r ^ d) * quarter + c * width)]

    def h_target(i):
        return u_home.at[pl.ds(pl.multiple_of(sub * rows, rows), rows), pl.ds(i * width, width)]

    def h_far(d, i, j):
        return pltpu.make_async_remote_copy(
            src_ref=h_source(d, i, j), dst_ref=h_target(i),
            send_sem=h_send.at[d, j * per + i], recv_sem=h_recv.at[sub * per + i],
            device_id={"fsdp": (r ^ d) * group + j}, device_id_type=MESH)

    def h_near(i, j):
        return pltpu.make_async_copy(h_source(0, i, j), h_target(i), h_recv.at[sub * per + i])

    def wait_bytes(ref, sem):
        pltpu.make_async_copy(ref, ref, sem).wait()

    order = list(range(replicas - 1, 0, -1))

    def send_local(i, j):
        @pl.when(jnp.logical_not(hub))
        def _():
            for d in order:
                rs_copy(d, i, j, local).start()

    def send_fold(i, j):
        @pl.when(hub)
        def _():
            for d in [0] + order[::-1]:
                side = (r ^ d) * group + j
                at = span(side * piece + i * width)
                wait_bytes(m_recv.at[:, at], m_arrived.at[side * per + i])
                if d:
                    delta = base_vm[:, at] - loc_vm[:, at].astype(jnp.float32)
                    fold[:, at] = (delta + fold_coef * m_recv[:, at].astype(jnp.float32)).astype(jnp.bfloat16)
                    rs_copy(d, i, j, fold).start()

    def reduce(i, j):
        c = j * per + i
        here = pl.ds(c * width, width)
        at = span(r * quarter + c * width)
        own_base = base_vm[:, at]
        total[...] = own_base - loc_vm[:, at].astype(jnp.float32)

        @pl.when(hub)
        def _():
            total[...] += fold_coef * m_recv[:, at].astype(jnp.float32)

        for d in order:
            rs_copy(d, i, j, local).wait_recv()
        summed = total[...]
        for d in range(1, replicas):
            came = loc_recv[d - 1, :, here].astype(jnp.float32)
            summed = summed + jnp.where((r ^ d) == line, came, own_base - came)
        scale = LEARN_RATE * (1.0 + MOMENTUM_COEF) / replicas
        u_own[:, here] = (scale * summed).astype(jnp.bfloat16)
        for d in order:
            ag_copy(d, i, j).start()

        @pl.when(jnp.logical_and(hub, sub != j))
        def _():
            h_far(0, i, j).start()

        @pl.when(jnp.logical_and(hub, sub == j))
        def _():
            h_near(i, j).start()

        out_copy(i, j).start()

    def out_copy(i, j):
        c = j * per + i
        return pltpu.make_async_copy(
            u_own.at[:, pl.ds(c * width, width)], gathered.at[:, span(r * quarter + c * width)], out_sem.at[c])

    def give_back(i, j):
        for d in order[::-1]:
            ag_copy(d, i, j).wait_recv()

            @pl.when(hub)
            def _():
                h_far(d, i, j).start()

    def send_momentum(i):
        for k in range(group):
            away = f != r * group + k

            @pl.when(away)
            def _():
                m_far(k, i).start()

            @pl.when(jnp.logical_not(away))
            def _():
                m_near(k, i).start()

    for s in range(max(AHEAD, M_AHEAD)):
        if s < min(M_AHEAD, per):
            send_momentum(s)
        if s < min(AHEAD, len(steps)):
            send_local(*steps[s])
    load_local.wait()
    load_base.wait()
    for s in range(len(steps) + LAG):
        if s % group == 0 and s // group + M_AHEAD < per:
            send_momentum(s // group + M_AHEAD)
        if s + AHEAD < len(steps):
            send_local(*steps[s + AHEAD])
        if s < len(steps):
            send_fold(*steps[s])
            reduce(*steps[s])
        if s >= LAG:
            give_back(*steps[s - LAG])

    for k in range(group):
        for i in range(per):
            wait_bytes(u_home.at[pl.ds(k * rows, rows), pl.ds(i * width, width)], h_recv.at[k * per + i])

            @pl.when(f != r * group + k)
            def _():
                m_far(k, i).wait_send()

    for i, j in steps:
        out_copy(i, j).wait()
        for d in order:
            rs_copy(d, i, j, local).wait_send()
            ag_copy(d, i, j).wait_send()

        @pl.when(hub)
        def _():
            for d in order:
                h_far(d, i, j).wait_send()

        @pl.when(jnp.logical_and(hub, sub != j))
        def _():
            h_far(0, i, j).wait_send()


def per_device(local_weights, base_weights, momentum):
    rows, cols = base_weights.shape
    replicas = lax.axis_size("replica")
    shards = lax.axis_size("fsdp")
    group = shards // replicas
    piece = momentum.shape[1]
    per = next(n for n in (7, 1) if piece % (n * LANES) == 0)
    chunks = group * per
    quarter = cols // replicas
    dma = pltpu.SemaphoreType.DMA
    gathered, u_home = pl.pallas_call(
        functools.partial(sync_kernel, replicas, shards, per),
        out_shape=(
            jax.ShapeDtypeStruct((rows, cols), jnp.bfloat16),
            jax.ShapeDtypeStruct(momentum.shape, jnp.bfloat16),
        ),
        in_specs=[pl.BlockSpec(memory_space=pl.ANY)] * 3,
        out_specs=(pl.BlockSpec(memory_space=pl.ANY),) * 2,
        scratch_shapes=[
            pltpu.VMEM((rows, cols), jnp.float32),
            pltpu.VMEM((rows, cols), jnp.bfloat16),
            pltpu.VMEM(momentum.shape, jnp.float32),
            pltpu.VMEM(momentum.shape, jnp.bfloat16),
            pltpu.VMEM((rows, cols), jnp.bfloat16),
            pltpu.VMEM((rows, cols), jnp.bfloat16),
            pltpu.VMEM((replicas - 1, rows, quarter), jnp.bfloat16),
            pltpu.VMEM((rows, quarter), jnp.bfloat16),
            pltpu.VMEM((rows, piece // per), jnp.float32),
            dma((replicas - 1, chunks)), dma((replicas - 1, chunks)),
            dma((group * per,)), dma((shards * per,)),
            dma((replicas - 1, chunks)), dma((replicas - 1, chunks)),
            dma((replicas, chunks)), dma((group * per,)),
            dma((3,)), dma((chunks,)),
        ],
        compiler_params=pltpu.CompilerParams(
            collective_id=0, has_side_effects=True, vmem_limit_bytes=48 * 1024 * 1024),
    )(local_weights[0], base_weights, momentum)
    new_weights = base_weights - gathered.astype(jnp.float32)
    new_momentum = (MOMENTUM_COEF * momentum + unscaled(u_home)) / (1.0 + MOMENTUM_COEF)
    return new_weights, new_momentum


def unscaled(update):
    return update.astype(jnp.float32) / LEARN_RATE


def solution(mesh):
    return jax.shard_map(
        per_device,
        mesh=mesh,
        in_specs=(P("replica", "fsdp", None), P("fsdp", None), P("replica", "fsdp")),
        out_specs=(P("fsdp", None), P("replica", "fsdp")),
        check_vma=False,
    )
```
